128 devices in a mesh: ws: 8 (over y_hi, z), seq: 16 (over x, y_lo, core).
Axes of the slice: x: 4, y: 4 (y_hi: 2, y_lo: 2; y = y_hi * 2 + y_lo), z: 4, core: 2. Of those that a mesh axis runs over, the one named last changes fastest.
Arguments:
- tokens: bfloat16 [8, 6144, 1536], P('ws', 'seq'), may hold values from -16 to 16
- w_same: bfloat16 [1536, 1536], replicated, may hold values from -0.15625 to 0.15625
- w_partner: bfloat16 [1536, 1536], replicated, may hold values from -0.15625 to 0.15625
- w_query: bfloat16 [1536, 1024], replicated, may hold values from -0.15625 to 0.15625
- w_key: bfloat16 [1536, 128], replicated, may hold values from -0.15625 to 0.15625
- w_value: bfloat16 [1536, 192], replicated, may hold values from -0.15625 to 0.15625
- w_out: bfloat16 [1536, 1536], replicated, may hold values from -0.15625 to 0.15625
Outputs:
- attended: bfloat16 [8, 6144, 1536], P('ws', 'seq')
The draws below stay inside these ranges and needn't reach their ends.
All inputs are finite; a program needn't handle non-finite values.
Results may differ from the reference program's by a relative error of at most 0.012.
Values may be sent and summed in bfloat16 or wider, within the bound.
A program may use at most 192 MiB of HBM per device.

```python
import jax
import jax.numpy as jnp
from jax import lax

D = 1536
HEADS = 8
DK = 128
DV = 192
TOK_DEV = 384
SEQ = 6144
LANES = 8
N_WS = 8
N_SEQ = 16


def draw_tokens(key, part):
    base_key = jax.random.fold_in(jax.random.fold_in(key, 17), 0)
    return jnp.clip(jax.random.normal(base_key, (LANES, SEQ, D)), -6.0, 6.0).astype(jnp.bfloat16)


def normal_values(rng, shape, scale, reach, held_as=jnp.bfloat16):
    result = jax.random.normal(rng, shape, jnp.float32) * scale
    return jnp.minimum(jnp.maximum(result, -reach), reach).astype(held_as)


def setup_inputs(seed: int = 0) -> dict:
    key_of = jax.random.split(jax.random.key(seed), 8)
    return {
        "tokens": draw_tokens(jax.random.fold_in(key_of[7], 71), 0),
        "w_same": normal_values(key_of[1], (D, D), D ** -0.5, 0.15625),
        "w_partner": normal_values(key_of[2], (D, D), D ** -0.5, 0.15625),
        "w_query": normal_values(key_of[3], (D, HEADS * DK), D ** -0.5, 0.15625),
        "w_key": normal_values(key_of[4], (D, DK), D ** -0.5, 0.15625),
        "w_value": normal_values(key_of[5], (D, DV), D ** -0.5, 0.15625),
        "w_out": normal_values(key_of[6], (HEADS * DV, D), (HEADS * DV) ** -0.5, 0.15625),
    }


def attend(query, key, value):
    blocks = query.reshape(N_SEQ, TOK_DEV, HEADS, DK).astype(jnp.float32)
    key_f = key.astype(jnp.float32)
    value_f = value.astype(jnp.float32)
    factor = DK ** -0.5

    def one_block(rows):
        scores = jnp.einsum('qhd,kd->qhk', rows, key_f) * factor
        peak = jnp.max(scores, axis=2, keepdims=True)
        weights = jnp.exp(scores - peak)
        total = jnp.sum(weights, axis=2, keepdims=True)
        rounded = lax.optimization_barrier(weights.astype(jnp.bfloat16)).astype(jnp.float32)
        summed = jnp.einsum('qhk,kd->qhd', rounded, value_f)
        return (summed / total).astype(jnp.bfloat16).reshape(TOK_DEV, HEADS * DV)

    return lax.map(one_block, blocks).reshape(SEQ, HEADS * DV)


def reference(tokens, w_same, w_partner, w_query, w_key, w_value, w_out):
    paired = tokens.reshape(N_WS // 2, 2, SEQ, D)[:, ::-1]
    mirrored = jnp.flip(paired, axis=2).reshape(N_WS * SEQ, D)
    flat = tokens.reshape(N_WS * SEQ, D)
    hidden = (jnp.dot(flat, w_same, preferred_element_type=jnp.float32)
              + jnp.dot(mirrored, w_partner, preferred_element_type=jnp.float32)).astype(jnp.bfloat16)
    query = jnp.dot(hidden, w_query, preferred_element_type=jnp.float32).astype(jnp.bfloat16)
    key = jnp.dot(hidden, w_key, preferred_element_type=jnp.float32).astype(jnp.bfloat16)
    value = jnp.dot(hidden, w_value, preferred_element_type=jnp.float32).astype(jnp.bfloat16)
    query = query.reshape(N_WS, SEQ, HEADS * DK)
    key = key.reshape(N_WS, SEQ, DK)
    value = value.reshape(N_WS, SEQ, DV)
    outputs = []
    for lane in range(N_WS):
        mixed = attend(query[lane], key[lane], value[lane])
        outputs.append(jnp.dot(mixed, w_out, preferred_element_type=jnp.float32).astype(jnp.bfloat16))
    return jnp.stack(outputs, axis=0)
```

```python
import functools
import math

import jax
import jax.numpy as jnp
from jax import lax
from jax.experimental import pallas as pl
from jax.experimental.pallas import tpu as pltpu
from jax.sharding import PartitionSpec as P

MESH = pl.DeviceIdType.MESH
F32 = jnp.float32
BF16 = jnp.bfloat16
NT = (((1,), (1,)), ((), ()))

Y, H, M = 1, 2, 4
ORDER = (0, H, Y, M, Y ^ H, M ^ H, Y ^ M, Y ^ M ^ H)
PLACE = {slot: place for place, slot in enumerate(ORDER)}
SENDS = ((0, Y), (0, M), (0, H), (Y, H), (M, H), (M, Y), (Y ^ M, H))


def kernel(
    dims,
    tok, w_same, w_partner, w_query, w_key, w_value_t, w_out,
    out_ref,
    tok_v, flip_v, same_v, partner_v, query_v, key_v, value_v, out_v, hid_v,
    kv_out, kv_in, kv_mine, kv_all, keys_v, vals_v,
    qb_out, qb_in, qa_v, q_v, peak_v, acc_v, sum_v,
    load_sem, pair_send, pair_recv, ring_send, ring_recv, core_send, core_recv,
):
    rows, width, heads, dk, dv = dims
    chunks = heads // 2
    half = rows // 2
    ws = lax.axis_index("ws")
    seq = lax.axis_index("seq")
    last = lax.axis_size("seq") - 1
    x, y, core = seq // 4, (seq // 2) % 2, seq % 2
    pair = {"ws": ws + 1 - 2 * (ws % 2), "seq": last - seq}
    other = {"ws": ws, "seq": seq + 1 - 2 * core}
    link = {
        Y: {"ws": ws, "seq": seq + 2 - 4 * y},
        H: {"ws": ws, "seq": seq + 4 - 8 * (x % 2)},
        M: {"ws": ws, "seq": (3 - x) * 4 + y * 2 + core},
    }

    loads = [pltpu.make_async_copy(tok.at[0], tok_v, load_sem.at[0])]
    tiles = width // 256
    for n in range(tiles):
        loads.append(pltpu.make_async_copy(w_partner.at[:, pl.ds(n * 256, 256)], partner_v.at[n], load_sem.at[1 + n]))
    base = 1 + tiles
    rest = (
        (w_key, key_v),
        (w_value_t, value_v.at[pl.ds(0, dv)]),
        (w_value_t.at[pl.ds(128, dv - 128)], value_v.at[pl.ds(dv, dv - 128)]),
    )
    for n, (src, dst) in enumerate(rest):
        loads.append(pltpu.make_async_copy(src, dst, load_sem.at[base + n]))
    q_base = base + len(rest)
    for n in range(chunks):
        loads.append(pltpu.make_async_copy(w_query.at[:, pl.ds(n * 256, 256)], query_v.at[n], load_sem.at[q_base + n]))
    s_base = q_base + chunks
    for n in range(tiles):
        loads.append(pltpu.make_async_copy(w_same.at[:, pl.ds(n * 256, 256)], same_v.at[n], load_sem.at[s_base + n]))
    o_base = s_base + tiles
    loads.append(pltpu.make_async_copy(w_out, out_v, load_sem.at[o_base]))
    for copy in loads:
        copy.start()

    barrier = pltpu.get_barrier_semaphore()
    for peer in (pair, other, link[Y], link[H], link[M]):
        pl.semaphore_signal(barrier, inc=1, device_id=peer, device_id_type=MESH)

    loads[0].wait()
    turned = lax.broadcasted_iota(jnp.int32, (rows, rows), 0) + lax.broadcasted_iota(jnp.int32, (rows, rows), 1)
    turn = jnp.where(turned == rows - 1, 1.0, 0.0).astype(BF16)
    for n in range(tiles):
        flip_v[:, n * 256:(n + 1) * 256] = jnp.dot(
            turn, tok_v[:, n * 256:(n + 1) * 256], preferred_element_type=F32
        ).astype(BF16)
    for n in range(tiles):
        loads[1 + n].wait()
        hid_v[:, n * 256:(n + 1) * 256] = jnp.dot(flip_v[...], partner_v[n], preferred_element_type=F32).astype(BF16)

    def key_value():
        hidden = hid_v[...]
        k = jnp.dot(hidden, key_v[...], preferred_element_type=F32)
        v = lax.dot_general(hidden, value_v[...], NT, preferred_element_type=F32)
        lane = lax.broadcasted_iota(jnp.int32, (half, 128), 1)
        tail = jnp.where(lane < dv - 128, v[:half, 128:], v[half:, 128:])
        return k, v[:, :128], tail

    for n in range(len(rest)):
        loads[base + n].wait()
    k, v, tail = key_value()
    kv_out[0:rows] = k.astype(BF16)
    kv_out[rows:2 * rows] = v.astype(BF16)
    kv_out[2 * rows:] = tail.astype(BF16)

    def query_out(n):
        loads[q_base + n].wait()
        q = jnp.dot(hid_v[...], query_v[n], preferred_element_type=F32).astype(BF16)
        qb_out[n, 0:rows] = q[:, :128]
        qb_out[n, rows:] = q[:, 128:]

    query_out(0)
    pl.semaphore_wait(barrier, 5)
    kv_copy = pltpu.make_async_remote_copy(
        src_ref=kv_out, dst_ref=kv_in, send_sem=pair_send.at[0], recv_sem=pair_recv.at[0],
        device_id=pair, device_id_type=MESH,
    )
    kv_copy.start()
    q_copies = [
        pltpu.make_async_remote_copy(
            src_ref=qb_out.at[n], dst_ref=qb_in.at[n], send_sem=pair_send.at[1 + n], recv_sem=pair_recv.at[1 + n],
            device_id=pair, device_id_type=MESH,
        )
        for n in range(chunks)
    ]
    for n in range(1, chunks):
        query_out(n)
    q_copies[0].start()

    for n in range(tiles):
        loads[s_base + n].wait()
        hid_v[:, n * 256:(n + 1) * 256] = jnp.dot(tok_v[...], same_v[n], preferred_element_type=F32).astype(BF16)
    k, v, tail = key_value()
    kv_mine[0:rows] = k
    kv_mine[rows:2 * rows] = v
    kv_mine[2 * rows:] = tail
    for n in range(chunks):
        q = jnp.dot(hid_v[...], query_v[n], preferred_element_type=F32)
        qa_v[n, 0:rows] = q[:, :128]
        qa_v[n, rows:] = q[:, 128:]

    kv_copy.wait_recv()
    kv_all[0, 0] = (kv_mine[...] + kv_in[...].astype(F32)).astype(BF16)

    ring = {}
    for n, (slot, l) in enumerate(SENDS):
        ring[slot, l] = pltpu.make_async_remote_copy(
            src_ref=kv_all.at[slot, 0], dst_ref=kv_all.at[slot ^ l, 0],
            send_sem=ring_send.at[n], recv_sem=ring_recv.at[slot ^ l],
            device_id=link[l], device_id_type=MESH,
        )
    came = {slot ^ l: copy for (slot, l), copy in ring.items()}
    cores = {
        slot: pltpu.make_async_remote_copy(
            src_ref=kv_all.at[slot, 0], dst_ref=kv_all.at[slot, 1],
            send_sem=core_send.at[slot], recv_sem=core_recv.at[slot],
            device_id=other, device_id_type=MESH,
        )
        for slot in range(8)
    }

    def unpack(place, slot):
        lane = lax.broadcasted_iota(jnp.int32, (half, 128), 1)
        for c in range(2):
            at = c * rows
            keys_v[place, at:at + rows] = kv_all[slot, c, 0:rows]
            vals_v[place, at:at + rows, 0:128] = kv_all[slot, c, rows:2 * rows]
            t = kv_all[slot, c, 2 * rows:].astype(F32)
            ones = jnp.where(lane == dv - 128, 1.0, 0.0)
            first = jnp.where(lane < dv - 128, t, ones)
            second = jnp.where(lane < dv - 128, pltpu.roll(t, 64, 1), ones)
            vals_v[place, at:at + half, 128:256] = first.astype(BF16)
            vals_v[place, at + half:at + rows, 128:256] = second.astype(BF16)

    def arrive(slot):
        came[slot].wait_recv()
        cores[slot].start()

    def stage(place):
        slot = ORDER[place]
        if place == 1:
            arrive(Y)
            ring[Y, H].start()
            arrive(M)
            ring[M, Y].start()
            ring[M, H].start()
            arrive(H)
            q_copies[2].start()
        if place == 4:
            arrive(Y ^ M)
            ring[Y ^ M, H].start()
            arrive(Y ^ H)
            q_copies[3].start()
        if place == 5:
            arrive(M ^ H)
        if place == 7:
            arrive(Y ^ M ^ H)
        cores[slot].wait_recv()
        unpack(place, slot)

    ring[0, Y].start()
    ring[0, M].start()
    ring[0, H].start()
    cores[0].start()
    q_copies[1].start()
    loads[o_base].wait()

    scale = dk ** -0.5 * math.log2(math.e)
    q_rows = 2 * rows
    step_keys = 2 * rows

    def chunk(c, carry):
        for n in range(chunks):
            @pl.when(c == n)
            def _():
                q_copies[n].wait_recv()
        q_v[...] = ((qa_v[c] + qb_in[c].astype(F32)) * scale).astype(BF16)
        peak_v[...] = jnp.full_like(peak_v, -jnp.inf)
        acc_v[...] = jnp.zeros_like(acc_v)

        def step(place, carry):
            for n in range(8):
                @pl.when((c == 0) & (place == n))
                def _():
                    stage(n)
            q = q_v[...]
            peak = peak_v[:, 0:1]
            acc = acc_v[...]
            for j in range(0, step_keys, 256):
                s = lax.dot_general(q, keys_v[place, j:j + 256], NT, preferred_element_type=F32)
                new = jnp.maximum(peak, jnp.max(s, axis=1, keepdims=True))
                weights = jnp.exp2(s - new).astype(BF16)
                acc = acc * jnp.exp2(peak - new) + jnp.dot(
                    weights, vals_v[place, j:j + 256], preferred_element_type=F32
                )
                peak = new
            peak_v[...] = jnp.broadcast_to(peak, peak_v.shape)
            acc_v[...] = acc
            return carry

        lax.fori_loop(0, 8, step, 0)
        total = acc_v[:, dv:dv + 1]
        for h in range(2):
            at = h * rows
            mixed = (acc_v[at:at + rows, 0:dv] / total[at:at + rows]).astype(BF16)
            w = out_v[pl.ds(pl.multiple_of((2 * c + h) * dv, dv), dv), :]
            part = jnp.dot(mixed, w, preferred_element_type=F32)
            if h == 0:
                first = part
        both = first + part

        @pl.when(c == 0)
        def _():
            sum_v[...] = both

        @pl.when(c > 0)
        def _():
            sum_v[...] += both
        return carry

    lax.fori_loop(0, chunks, chunk, 0)
    out_ref[0] = sum_v[...].astype(BF16)

    kv_copy.wait_send()
    for copy in q_copies:
        copy.wait_send()
    for copy in ring.values():
        copy.wait_send()
    for copy in cores.values():
        copy.wait_send()


def body(tokens, w_same, w_partner, w_query, w_key, w_value, w_out):
    _, rows, width = tokens.shape
    dk, dv = w_key.shape[1], w_value.shape[1]
    heads = w_query.shape[1] // dk
    chunks, tiles, pack = heads // 2, width // 256, 2 * rows + rows // 2
    dma = pltpu.SemaphoreType.DMA
    anyspace = pl.BlockSpec(memory_space=pl.ANY)
    return pl.pallas_call(
        functools.partial(kernel, (rows, width, heads, dk, dv)),
        out_shape=jax.ShapeDtypeStruct((1, rows, width), BF16),
        in_specs=[anyspace] * 7,
        out_specs=pl.BlockSpec(memory_space=pltpu.VMEM),
        scratch_shapes=[
            pltpu.VMEM((rows, width), BF16),
            pltpu.VMEM((rows, width), BF16),
            pltpu.VMEM((tiles, width, 256), BF16),
            pltpu.VMEM((tiles, width, 256), BF16),
            pltpu.VMEM((chunks, width, 256), BF16),
            pltpu.VMEM((width, dk), BF16),
            pltpu.VMEM((256, width), BF16),
            pltpu.VMEM((heads * dv, width), BF16),
            pltpu.VMEM((rows, width), BF16),
            pltpu.VMEM((pack, 128), BF16),
            pltpu.VMEM((pack, 128), BF16),
            pltpu.VMEM((pack, 128), F32),
            pltpu.VMEM((8, 2, pack, 128), BF16),
            pltpu.VMEM((8, 2 * rows, 128), BF16),
            pltpu.VMEM((8, 2 * rows, 256), BF16),
            pltpu.VMEM((chunks, 2 * rows, 128), BF16),
            pltpu.VMEM((chunks, 2 * rows, 128), BF16),
            pltpu.VMEM((chunks, 2 * rows, 128), F32),
            pltpu.VMEM((2 * rows, 128), BF16),
            pltpu.VMEM((2 * rows, 128), F32),
            pltpu.VMEM((2 * rows, 256), F32),
            pltpu.VMEM((rows, width), F32),
            dma((1 + 2 * tiles + 3 + chunks + 1,)),
            dma((1 + chunks,)),
            dma((1 + chunks,)),
            dma((len(SENDS),)),
            dma((8,)),
            dma((8,)),
            dma((8,)),
        ],
        compiler_params=pltpu.CompilerParams(
            collective_id=0, has_side_effects=True, vmem_limit_bytes=62 << 20
        ),
        name="strand_attention",
    )(tokens, w_same, w_partner, w_query, w_key, w_value.T, w_out)


def solution(mesh):
    placed = (P("ws", "seq", None), P(), P(), P(), P(), P(), P())
    return jax.shard_map(
        body, mesh=mesh, in_specs=placed, out_specs=P("ws", "seq", None), check_vma=False
    )
```

```python
import functools
import math

import jax
import jax.numpy as jnp
from jax import lax
from jax.experimental import pallas as pl
from jax.experimental.pallas import tpu as pltpu
from jax.sharding import PartitionSpec as P

MESH = pl.DeviceIdType.MESH
F32 = jnp.float32
BF16 = jnp.bfloat16
NT = (((1,), (1,)), ((), ()))
VMEM_LIMIT = 50 << 20
PIECE = 512

Y, H, M = 1, 2, 4
ORDER = (0, H, Y, M, Y ^ H, M ^ H, Y ^ M, Y ^ M ^ H)
PLACE = {slot: place for place, slot in enumerate(ORDER)}
SENDS = ((0, H, 0, 2), (0, Y, 0, 2), (0, M, 0, 2), (Y, H, 0, 2), (M, H, 0, 2), (M, Y, 0, 1), (Y, M, 1, 2), (Y ^ M, H, 0, 2))


def kernel(
    dims,
    tok, w_same, w_partner, w_query, w_key, w_value_t,
    out_ref,
    tok_v, same_v, partner_v, query_v, key_v, value_v, hid_v,
    kv_out, kv_in, kv_mine, kv_all, keys_v, vals_v,
    qb_out, qb_in, qa_v, q_v, peak_v, acc_v,
    load_sem, pair_send, pair_recv, ring_send, ring_recv, core_send, core_recv,
):
    rows, width, heads, dk, dv = dims
    chunks = heads // 2
    half = rows // 2
    pack = 2 * rows + half
    ws = lax.axis_index("ws")
    seq = lax.axis_index("seq")
    last = lax.axis_size("seq") - 1
    x, y, core = seq // 4, (seq // 2) % 2, seq % 2
    pair = {"ws": ws + 1 - 2 * (ws % 2), "seq": last - seq}
    other = {"ws": ws, "seq": seq + 1 - 2 * core}
    link = {
        Y: {"ws": ws, "seq": seq + 2 - 4 * y},
        H: {"ws": ws, "seq": seq + 4 - 8 * (x % 2)},
        M: {"ws": ws, "seq": (3 - x) * 4 + y * 2 + core},
    }

    tiles = width // PIECE
    tail_rows = dv - 128
    sources = [(tok.at[0], tok_v)]
    sources += [(w_partner.at[:, pl.ds(n * PIECE, PIECE)], partner_v.at[n]) for n in range(tiles)]
    sources += [
        (w_key, key_v),
        (w_value_t, value_v.at[pl.ds(0, dv)]),
        (w_value_t.at[pl.ds(128, tail_rows)], value_v.at[pl.ds(dv, tail_rows)]),
    ]
    sources += [(w_query, query_v), (w_same, same_v)]
    loads = [pltpu.make_async_copy(src, dst, load_sem.at[n]) for n, (src, dst) in enumerate(sources)]
    kv_base = 1 + tiles
    q_base = kv_base + 3
    s_base = q_base + 1

    def begin(first, stop):
        for copy in loads[first:stop]:
            copy.start()

    begin(0, q_base)
    barrier = pltpu.get_barrier_semaphore()
    for peer in (pair, other, link[Y], link[H], link[M]):
        pl.semaphore_signal(barrier, inc=1, device_id=peer, device_id_type=MESH)

    turned = lax.broadcasted_iota(jnp.int32, (rows, rows), 0) + lax.broadcasted_iota(jnp.int32, (rows, rows), 1)
    turn = jnp.where(turned == rows - 1, 1.0, 0.0).astype(BF16)

    def key_value():
        h = hid_v[...]
        k = jnp.dot(h, key_v[...], preferred_element_type=F32)
        v = lax.dot_general(h, value_v[...], NT, preferred_element_type=F32)
        return k, v

    def tail(v):
        lane = lax.broadcasted_iota(jnp.int32, (half, 128), 1)
        return jnp.where(lane < tail_rows, v[:half, 128:], v[half:, 128:])

    with jax.named_scope("w_tok"):
        loads[0].wait()
    with jax.named_scope("hB"):
        for n in range(tiles):
            loads[1 + n].wait()
            part = jnp.dot(tok_v[...], partner_v[n], preferred_element_type=F32)
            hid_v[:, n * PIECE:(n + 1) * PIECE] = part.astype(BF16)
            if n == 0:
                begin(q_base, s_base)
    begin(s_base, len(loads))
    with jax.named_scope("kvB"):
        for n in range(3):
            loads[kv_base + n].wait()
        k, v = key_value()
        both = jnp.concatenate([k, v], axis=1).astype(BF16)
        both = jnp.dot(turn, both, preferred_element_type=F32)
        kv_out[0:rows] = both[:, 0:128].astype(BF16)
        kv_out[rows:2 * rows] = both[:, 128:256].astype(BF16)
        kv_out[2 * rows:] = tail(both[:, 128:]).astype(BF16)

    kv_copy = pltpu.make_async_remote_copy(
        src_ref=kv_out, dst_ref=kv_in, send_sem=pair_send.at[0], recv_sem=pair_recv.at[0],
        device_id=pair, device_id_type=MESH,
    )
    q_copies = [
        pltpu.make_async_remote_copy(
            src_ref=qb_out.at[n], dst_ref=qb_in.at[n], send_sem=pair_send.at[1 + n], recv_sem=pair_recv.at[1 + n],
            device_id=pair, device_id_type=MESH,
        )
        for n in range(chunks)
    ]
    with jax.named_scope("barrier"):
        pl.semaphore_wait(barrier, 5)
    kv_copy.start()

    def heads_of(q):
        for n in range(heads):
            at = (n % 2) * rows
            yield n // 2, slice(at, at + rows), q[:, n * dk:(n + 1) * dk]

    with jax.named_scope("qB"):
        loads[q_base].wait()
        q = jnp.dot(hid_v[...], query_v[...], preferred_element_type=F32).astype(BF16)
        q = jnp.dot(turn, q, preferred_element_type=F32).astype(BF16)
        for n, at, part in heads_of(q):
            qb_out[n, at] = part

    with jax.named_scope("hA"):
        loads[s_base].wait()
        q_copies[0].start()
        hid_v[...] = jnp.dot(tok_v[...], same_v[...], preferred_element_type=F32).astype(BF16)
    with jax.named_scope("kvA"):
        k, v = key_value()
        kv_mine[0:rows] = k
        kv_mine[rows:2 * rows] = v[:, :128]
        kv_mine[2 * rows:] = tail(v)
    with jax.named_scope("qA"):
        q = jnp.dot(hid_v[...], query_v[...], preferred_element_type=F32)
        for n, at, part in heads_of(q):
            qa_v[n, at] = part

    with jax.named_scope("w_kv"):
        kv_copy.wait_recv()
    kv_all[0, 0] = (kv_mine[...] + kv_in[...].astype(F32)).astype(BF16)

    ring, came = {}, {slot: [] for slot in range(8)}
    for n, (slot, l, first, stop) in enumerate(SENDS):
        part = pl.ds(first * pack // 2, (stop - first) * pack // 2)
        ring[slot, l] = pltpu.make_async_remote_copy(
            src_ref=kv_all.at[slot, 0, part], dst_ref=kv_all.at[slot ^ l, 0, part],
            send_sem=ring_send.at[n], recv_sem=ring_recv.at[n],
            device_id=link[l], device_id_type=MESH,
        )
        came[slot ^ l].append(ring[slot, l])
    cores = {
        slot: pltpu.make_async_remote_copy(
            src_ref=kv_all.at[slot, 0], dst_ref=kv_all.at[slot, 1],
            send_sem=core_send.at[slot], recv_sem=core_recv.at[slot],
            device_id=other, device_id_type=MESH,
        )
        for slot in range(8)
    }

    def unpack(slot, c):
        place = PLACE[slot]
        lane = lax.broadcasted_iota(jnp.int32, (half, 128), 1)
        at = c * rows
        keys_v[place, at:at + rows] = kv_all[slot, c, 0:rows]
        vals_v[place, at:at + rows, 0:128] = kv_all[slot, c, rows:2 * rows]
        t = kv_all[slot, c, 2 * rows:].astype(F32)
        ones = jnp.where(lane == tail_rows, 1.0, 0.0)
        first = jnp.where(lane < tail_rows, t, ones)
        second = jnp.where(lane < tail_rows, pltpu.roll(t, 64, 1), ones)
        vals_v[place, at:at + half, 128:256] = first.astype(BF16)
        vals_v[place, at + half:at + rows, 128:256] = second.astype(BF16)

    def arrive(slot, *onward):
        with jax.named_scope(f"w_slot{slot}"):
            for copy in came[slot]:
                copy.wait_recv()
        cores[slot].start()
        for l in onward:
            ring[slot, l].start()
        unpack(slot, 0)

    def complete(slot):
        with jax.named_scope(f"w_core{slot}"):
            cores[slot].wait_recv()
        unpack(slot, 1)

    def stage(place):
        if place == 1:
            arrive(H)
            arrive(Y, H)
            arrive(M, H)
            q_copies[2].start()
            ring[M, Y].start()
            ring[Y, M].start()
            q_copies[3].start()
        complete(ORDER[place])

    scale = dk ** -0.5 * math.log2(math.e)

    def query(c):
        for n in range(chunks):
            @pl.when(c == n)
            def _():
                with jax.named_scope(f"w_q{n}"):
                    q_copies[n].wait_recv()
        q_v[c] = ((qa_v[c] + qb_in[c].astype(F32)) * scale).astype(BF16)

    def attend(q, places, peak, acc):
        for place in places:
            for j in range(0, 2 * rows, 256):
                s = lax.dot_general(q, keys_v[place, j:j + 256], NT, preferred_element_type=F32)
                new = jnp.maximum(peak, jnp.broadcast_to(jnp.max(s, axis=1, keepdims=True), peak.shape))
                weights = jnp.concatenate([jnp.exp2(s[:, :128] - new), jnp.exp2(s[:, 128:] - new)], axis=1).astype(BF16)
                keep = jnp.exp2(peak - new)
                acc = acc * jnp.concatenate([keep, keep], axis=1) + jnp.dot(
                    weights, vals_v[place, j:j + 256], preferred_element_type=F32
                )
                peak = new
        return peak, acc

    unpack(0, 0)
    ring[0, H].start()
    ring[0, Y].start()
    ring[0, M].start()
    cores[0].start()
    q_copies[1].start()

    query(0)
    peak_v[0] = jnp.full(peak_v.shape[1:], -jnp.inf, F32)
    acc_v[0] = jnp.zeros(acc_v.shape[1:], F32)

    def early(place, carry):
        for n in range(4):
            @pl.when(place == n)
            def _():
                stage(n)
        with jax.named_scope("early"):
            peak_v[0], acc_v[0] = attend(q_v[0], (place,), peak_v[0], acc_v[0])
        return carry

    lax.fori_loop(0, 4, early, 0)

    def near(c, carry):
        query(c)
        with jax.named_scope("near"):
            start = jnp.full(peak_v.shape[1:], -jnp.inf, F32), jnp.zeros(acc_v.shape[1:], F32)
            peak_v[c], acc_v[c] = attend(q_v[c], range(4), *start)
        return carry

    lax.fori_loop(1, chunks - 1, near, 0)

    arrive(Y ^ H)
    arrive(M ^ H)
    complete(Y ^ H)
    complete(M ^ H)

    def middle(c, carry):
        with jax.named_scope("mid"):
            peak_v[c], acc_v[c] = attend(q_v[c], (4, 5), peak_v[c], acc_v[c])
        return carry

    lax.fori_loop(0, chunks - 1, middle, 0)
    arrive(Y ^ M, H)
    near(chunks - 1, 0)
    complete(Y ^ M)

    def store(c, acc):
        mixed = acc * (1.0 / acc[:, dv:dv + 1])
        lane = lax.broadcasted_iota(jnp.int32, (rows, 128), 1)
        a, b = mixed[:rows], mixed[rows:]
        turned_b = pltpu.roll(b[:, :128], 64, 1)
        inner = jnp.where(lane < 64, a[:, 128:], turned_b)
        end = jnp.where(lane < 64, turned_b, pltpu.roll(b[:, 128:], 64, 1))
        at = pl.multiple_of(c * 2 * dv, 128)
        out_ref[:, pl.ds(at, 2 * dv)] = jnp.concatenate([a[:, :128], inner, end], axis=1).astype(BF16)

    def far(k, carry):
        c = (k + chunks - 1) % chunks
        place = 4 + 2 * ((k + chunks - 1) // chunks)

        @pl.when(k == 1)
        def _():
            arrive(Y ^ M ^ H)
            complete(Y ^ M ^ H)

        with jax.named_scope("far"):
            peak_v[c], acc_v[c] = attend(q_v[c], (place, place + 1), peak_v[c], acc_v[c])

        @pl.when(k > 0)
        def _():
            store(c, acc_v[c])
        return carry

    lax.fori_loop(0, chunks + 1, far, 0)

    kv_copy.wait_send()
    for copy in q_copies:
        copy.wait_send()
    for copy in ring.values():
        copy.wait_send()
    for copy in cores.values():
        copy.wait_send()


def body(tokens, w_same, w_partner, w_query, w_key, w_value, w_out):
    _, rows, width = tokens.shape
    dk, dv = w_key.shape[1], w_value.shape[1]
    heads = w_query.shape[1] // dk
    chunks, tiles, pack = heads // 2, width // PIECE, 2 * rows + rows // 2
    dma = pltpu.SemaphoreType.DMA
    in_hbm = pl.BlockSpec(memory_space=pltpu.HBM)
    mixed = pl.pallas_call(
        functools.partial(kernel, (rows, width, heads, dk, dv)),
        out_shape=jax.ShapeDtypeStruct((rows, heads * dv), BF16),
        in_specs=[in_hbm] * 6,
        out_specs=pl.BlockSpec(memory_space=pltpu.VMEM),
        scratch_shapes=[
            pltpu.VMEM((rows, width), BF16),
            pltpu.VMEM((width, width), BF16),
            pltpu.VMEM((tiles, width, PIECE), BF16),
            pltpu.VMEM((width, heads * dk), BF16),
            pltpu.VMEM((width, dk), BF16),
            pltpu.VMEM((256, width), BF16),
            pltpu.VMEM((rows, width), BF16),
            pltpu.VMEM((pack, 128), BF16),
            pltpu.VMEM((pack, 128), BF16),
            pltpu.VMEM((pack, 128), F32),
            pltpu.VMEM((8, 2, pack, 128), BF16),
            pltpu.VMEM((8, 2 * rows, 128), BF16),
            pltpu.VMEM((8, 2 * rows, 256), BF16),
            pltpu.VMEM((chunks, 2 * rows, 128), BF16),
            pltpu.VMEM((chunks, 2 * rows, 128), BF16),
            pltpu.VMEM((chunks, 2 * rows, 128), F32),
            pltpu.VMEM((chunks, 2 * rows, 128), BF16),
            pltpu.VMEM((chunks, 2 * rows, 128), F32),
            pltpu.VMEM((chunks, 2 * rows, 256), F32),
            dma((1 + tiles + 5,)),
            dma((1 + chunks,)),
            dma((1 + chunks,)),
            dma((len(SENDS),)),
            dma((len(SENDS),)),
            dma((8,)),
            dma((8,)),
        ],
        compiler_params=pltpu.CompilerParams(
            collective_id=0, has_side_effects=True, vmem_limit_bytes=VMEM_LIMIT
        ),
        name="strand_attention",
    )(*(pltpu.with_memory_space_constraint(a, pltpu.HBM) for a in (tokens, w_same, w_partner, w_query, w_key, w_value.T)))
    return jnp.dot(mixed, w_out, preferred_element_type=F32).astype(BF16)[None]


def solution(mesh):
    placed = (P("ws", "seq", None), P(), P(), P(), P(), P(), P())
    return jax.shard_map(
        body, mesh=mesh, in_specs=placed, out_specs=P("ws", "seq", None), check_vma=False
    )
```

```python
import functools
import math

import jax
import jax.numpy as jnp
from jax import lax
from jax.experimental import pallas as pl
from jax.experimental.pallas import tpu as pltpu
from jax.sharding import PartitionSpec as P

MESH = pl.DeviceIdType.MESH
F32 = jnp.float32
BF16 = jnp.bfloat16
NT = (((1,), (1,)), ((), ()))
VMEM_LIMIT = 50 << 20
PIECE = 512

Y, H, M = 1, 2, 4
ORDER = (0, H, Y, M, Y ^ H, M ^ H, Y ^ M, Y ^ M ^ H)
PLACE = {slot: place for place, slot in enumerate(ORDER)}
SENDS = ((0, H, 0, 2), (0, Y, 0, 2), (0, M, 0, 2), (Y, H, 0, 2), (M, H, 0, 2), (M, Y, 0, 1), (Y, M, 1, 2), (Y ^ M, H, 0, 2))


def kernel(
    dims,
    tok, w_same, w_partner, w_query, w_key, w_value_t,
    out_ref,
    tok_v, same_v, partner_v, query_v, key_v, value_v, hid_v,
    kv_out, kv_in, kv_mine, kv_all, keys_v, vals_v,
    qb_out, qb_in, qa_v, q_v, peak_v, acc_v,
    load_sem, pair_send, pair_recv, ring_send, ring_recv, core_send, core_recv,
):
    rows, width, heads, dk, dv = dims
    chunks = heads // 2
    half = rows // 2
    pack = 2 * rows + half
    ws = lax.axis_index("ws")
    seq = lax.axis_index("seq")
    last = lax.axis_size("seq") - 1
    x, y, core = seq // 4, (seq // 2) % 2, seq % 2
    pair = {"ws": ws + 1 - 2 * (ws % 2), "seq": last - seq}
    other = {"ws": ws, "seq": seq + 1 - 2 * core}
    link = {
        Y: {"ws": ws, "seq": seq + 2 - 4 * y},
        H: {"ws": ws, "seq": seq + 4 - 8 * (x % 2)},
        M: {"ws": ws, "seq": (3 - x) * 4 + y * 2 + core},
    }

    tiles = width // PIECE
    tail_rows = dv - 128
    sources = [(tok.at[0], tok_v)]
    sources += [(w_partner.at[:, pl.ds(n * PIECE, PIECE)], partner_v.at[n]) for n in range(tiles)]
    sources += [
        (w_key, key_v),
        (w_value_t, value_v.at[pl.ds(0, dv)]),
        (w_value_t.at[pl.ds(128, tail_rows)], value_v.at[pl.ds(dv, tail_rows)]),
    ]
    sources += [(w_query, query_v), (w_same, same_v)]
    loads = [pltpu.make_async_copy(src, dst, load_sem.at[n]) for n, (src, dst) in enumerate(sources)]
    kv_base = 1 + tiles
    q_base = kv_base + 3
    s_base = q_base + 1

    def begin(first, stop):
        for copy in loads[first:stop]:
            copy.start()

    begin(0, q_base)
    barrier = pltpu.get_barrier_semaphore()
    for peer in (pair, other, link[Y], link[H], link[M]):
        pl.semaphore_signal(barrier, inc=1, device_id=peer, device_id_type=MESH)

    turned = lax.broadcasted_iota(jnp.int32, (rows, rows), 0) + lax.broadcasted_iota(jnp.int32, (rows, rows), 1)
    turn = jnp.where(turned == rows - 1, 1.0, 0.0).astype(BF16)

    def key(h):
        return jnp.dot(h, key_v[...], preferred_element_type=F32)

    def value(h):
        return lax.dot_general(h, value_v[...], NT, preferred_element_type=F32)

    def tail(v):
        lane = lax.broadcasted_iota(jnp.int32, (half, 128), 1)
        return jnp.where(lane < tail_rows, v[:half, 128:], v[half:, 128:])

    with jax.named_scope("w_tok"):
        loads[0].wait()
    with jax.named_scope("hB"):
        for n in range(tiles):
            loads[1 + n].wait()
            part = jnp.dot(tok_v[...], partner_v[n], preferred_element_type=F32)
            hid_v[:, n * PIECE:(n + 1) * PIECE] = part.astype(BF16)
            if n == 0:
                begin(q_base, s_base)
    begin(s_base, len(loads))
    def to_pair(src, dst, n):
        return pltpu.make_async_remote_copy(
            src_ref=src, dst_ref=dst, send_sem=pair_send.at[n], recv_sem=pair_recv.at[n],
            device_id=pair, device_id_type=MESH,
        )

    kv_parts = (pl.ds(0, rows), pl.ds(rows, pack - rows))
    kv_copies = [to_pair(kv_out.at[part], kv_in.at[part], n) for n, part in enumerate(kv_parts)]
    q_copies = [to_pair(qb_out.at[n], qb_in.at[n], 2 + n) for n in range(chunks)]
    with jax.named_scope("kB"):
        for n in range(3):
            loads[kv_base + n].wait()
        kv_out[0:rows] = key(hid_v[...]).astype(BF16)
    with jax.named_scope("barrier"):
        pl.semaphore_wait(barrier, 5)
    kv_copies[0].start()
    with jax.named_scope("vB"):
        v = value(hid_v[...])
        kv_out[rows:2 * rows] = v[:, :128].astype(BF16)
        kv_out[2 * rows:] = tail(v).astype(BF16)
    kv_copies[1].start()

    def heads_of(q):
        for n in range(heads):
            at = (n % 2) * rows
            yield n // 2, slice(at, at + rows), q[:, n * dk:(n + 1) * dk]

    with jax.named_scope("qB"):
        loads[q_base].wait()
        q = jnp.dot(hid_v[...], query_v[...], preferred_element_type=F32).astype(BF16)
        q = jnp.dot(turn, q, preferred_element_type=F32).astype(BF16)
        for n, at, part in heads_of(q):
            qb_out[n, at] = part

    with jax.named_scope("hA"):
        loads[s_base].wait()
        q_copies[0].start()
        hid_v[...] = jnp.dot(tok_v[...], same_v[...], preferred_element_type=F32).astype(BF16)
    with jax.named_scope("kvA"):
        turned_hid = jnp.dot(turn, hid_v[...], preferred_element_type=F32).astype(BF16)
        kv_mine[0:rows] = key(turned_hid)
        v = value(turned_hid)
        kv_mine[rows:2 * rows] = v[:, :128]
        kv_mine[2 * rows:] = tail(v)
    with jax.named_scope("qA"):
        q = jnp.dot(hid_v[...], query_v[...], preferred_element_type=F32)
        for n, at, part in heads_of(q):
            qa_v[n, at] = part

    with jax.named_scope("w_kv"):
        for copy in kv_copies:
            copy.wait_recv()
    kv_all[0, 0] = (kv_mine[...] + kv_in[...].astype(F32)).astype(BF16)

    ring, came = {}, {slot: [] for slot in range(8)}
    for n, (slot, l, first, stop) in enumerate(SENDS):
        part = pl.ds(first * pack // 2, (stop - first) * pack // 2)
        ring[slot, l] = pltpu.make_async_remote_copy(
            src_ref=kv_all.at[slot, 0, part], dst_ref=kv_all.at[slot ^ l, 0, part],
            send_sem=ring_send.at[n], recv_sem=ring_recv.at[n],
            device_id=link[l], device_id_type=MESH,
        )
        came[slot ^ l].append(ring[slot, l])
    cores = {
        slot: pltpu.make_async_remote_copy(
            src_ref=kv_all.at[slot, 0], dst_ref=kv_all.at[slot, 1],
            send_sem=core_send.at[slot], recv_sem=core_recv.at[slot],
            device_id=other, device_id_type=MESH,
        )
        for slot in range(8)
    }

    def unpack(slot, c):
        place, at = PLACE[slot], c * rows
        if slot in (Y, M):
            place, at = 2 + c, rows * (slot == M)
        lane = lax.broadcasted_iota(jnp.int32, (half, 128), 1)
        keys_v[place, at:at + rows] = kv_all[slot, c, 0:rows]
        vals_v[place, at:at + rows, 0:128] = kv_all[slot, c, rows:2 * rows]
        t = kv_all[slot, c, 2 * rows:].astype(F32)
        ones = jnp.where(lane == tail_rows, 1.0, 0.0)
        first = jnp.where(lane < tail_rows, t, ones)
        second = jnp.where(lane < tail_rows, pltpu.roll(t, 64, 1), ones)
        vals_v[place, at:at + half, 128:256] = first.astype(BF16)
        vals_v[place, at + half:at + rows, 128:256] = second.astype(BF16)

    def arrive(slot, *onward):
        with jax.named_scope(f"w_slot{slot}"):
            for copy in came[slot]:
                copy.wait_recv()
        cores[slot].start()
        for l in onward:
            ring[slot, l].start()
        unpack(slot, 0)

    def complete(slot):
        with jax.named_scope(f"w_core{slot}"):
            cores[slot].wait_recv()
        unpack(slot, 1)

    def stage(place):
        if place == 0:
            complete(0)
        if place == 1:
            arrive(H)
            complete(H)
            arrive(Y, H)
            arrive(M, H)
            ring[M, Y].start()
            ring[Y, M].start()
            q_copies[3].start()
        if place == 3:
            complete(Y)
            complete(M)

    scale = dk ** -0.5 * math.log2(math.e)

    def query(c):
        if isinstance(c, int):
            with jax.named_scope(f'w_q{c}'):
                q_copies[c].wait_recv()
        else:
            for n in range(2, chunks):
                @pl.when(c == n)
                def _():
                    with jax.named_scope(f"w_q{n}"):
                        q_copies[n].wait_recv()
        q_v[c] = ((qa_v[c] + qb_in[c].astype(F32)) * scale).astype(BF16)

    def attend(q, places, peak, acc):
        for place in places:
            for j in range(0, 2 * rows, 256):
                s = lax.dot_general(q, keys_v[place, j:j + 256], NT, preferred_element_type=F32)
                new = jnp.maximum(peak, jnp.broadcast_to(jnp.max(s, axis=1, keepdims=True), peak.shape))
                weights = jnp.concatenate([jnp.exp2(s[:, :128] - new), jnp.exp2(s[:, 128:] - new)], axis=1).astype(BF16)
                keep = jnp.exp2(peak - new)
                acc = acc * jnp.concatenate([keep, keep], axis=1) + jnp.dot(
                    weights, vals_v[place, j:j + 256], preferred_element_type=F32
                )
                peak = new
        return peak, acc

    unpack(0, 0)
    ring[0, H].start()
    ring[0, Y].start()
    ring[0, M].start()
    cores[0].start()
    q_copies[1].start()
    q_copies[2].start()

    query(0)
    peak_v[0] = jnp.full(peak_v.shape[1:], -jnp.inf, F32)
    acc_v[0] = jnp.zeros(acc_v.shape[1:], F32)

    def early(place, carry):
        for n in range(4):
            @pl.when(place == n)
            def _():
                stage(n)
        with jax.named_scope("early"):
            peak_v[0], acc_v[0] = attend(q_v[0], (place,), peak_v[0], acc_v[0])
        return carry

    lax.fori_loop(0, 4, early, 0)

    def one(c, place):
        with jax.named_scope("one"):
            peak_v[c], acc_v[c] = attend(q_v[c], (place,), peak_v[c], acc_v[c])

    def begin_chunk(c, places):
        with jax.named_scope("near"):
            start = jnp.full(peak_v.shape[1:], -jnp.inf, F32), jnp.zeros(acc_v.shape[1:], F32)
            peak_v[c], acc_v[c] = attend(q_v[c], places, *start)

    def second(c, carry):
        one(c, PLACE[Y ^ H])
        return carry

    def late(c, carry):
        query(c)

        @pl.when(c == chunks - 2)
        def _():
            complete(Y ^ H)

        begin_chunk(c, range(5))

        @pl.when(c == chunks - 2)
        def _():
            arrive(Y ^ M, H)
            arrive(M ^ H)
            lax.fori_loop(0, chunks - 2, second, 0)
        return carry

    query(1)
    begin_chunk(1, range(4))
    arrive(Y ^ H)
    lax.fori_loop(2, chunks, late, 0)
    complete(M ^ H)
    complete(Y ^ M)
    arrive(Y ^ M ^ H)
    with jax.named_scope("two"):
        peak_v[0], acc_v[0] = attend(q_v[0], (5, 6), peak_v[0], acc_v[0])
    complete(Y ^ M ^ H)
    one(0, 7)

    def store(c, acc):
        mixed = acc * (1.0 / acc[:, dv:dv + 1])
        lane = lax.broadcasted_iota(jnp.int32, (rows, 128), 1)
        a, b = mixed[:rows], mixed[rows:]
        turned_b = pltpu.roll(b[:, :128], 64, 1)
        inner = jnp.where(lane < 64, a[:, 128:], turned_b)
        end = jnp.where(lane < 64, turned_b, pltpu.roll(b[:, 128:], 64, 1))
        at = pl.multiple_of(c * 2 * dv, 128)
        out_ref[:, pl.ds(at, 2 * dv)] = jnp.concatenate([a[:, :128], inner, end], axis=1).astype(BF16)

    def far(c, carry):
        with jax.named_scope("far"):
            store(c - 1, acc_v[c - 1])
            _, acc_v[c] = attend(q_v[c], range(5, 8), peak_v[c], acc_v[c])
        return carry

    lax.fori_loop(1, chunks, far, 0)
    store(chunks - 1, acc_v[chunks - 1])

    for copy in kv_copies + q_copies:
        copy.wait_send()
    for copy in ring.values():
        copy.wait_send()
    for copy in cores.values():
        copy.wait_send()


def body(tokens, w_same, w_partner, w_query, w_key, w_value, w_out):
    _, rows, width = tokens.shape
    dk, dv = w_key.shape[1], w_value.shape[1]
    heads = w_query.shape[1] // dk
    chunks, tiles, pack = heads // 2, width // PIECE, 2 * rows + rows // 2
    dma = pltpu.SemaphoreType.DMA
    in_hbm = pl.BlockSpec(memory_space=pltpu.HBM)
    mixed = pl.pallas_call(
        functools.partial(kernel, (rows, width, heads, dk, dv)),
        out_shape=jax.ShapeDtypeStruct((rows, heads * dv), BF16),
        in_specs=[in_hbm] * 6,
        out_specs=pl.BlockSpec(memory_space=pltpu.VMEM),
        scratch_shapes=[
            pltpu.VMEM((rows, width), BF16),
            pltpu.VMEM((width, width), BF16),
            pltpu.VMEM((tiles, width, PIECE), BF16),
            pltpu.VMEM((width, heads * dk), BF16),
            pltpu.VMEM((width, dk), BF16),
            pltpu.VMEM((256, width), BF16),
            pltpu.VMEM((rows, width), BF16),
            pltpu.VMEM((pack, 128), BF16),
            pltpu.VMEM((pack, 128), BF16),
            pltpu.VMEM((pack, 128), F32),
            pltpu.VMEM((8, 2, pack, 128), BF16),
            pltpu.VMEM((8, 2 * rows, 128), BF16),
            pltpu.VMEM((8, 2 * rows, 256), BF16),
            pltpu.VMEM((chunks, 2 * rows, 128), BF16),
            pltpu.VMEM((chunks, 2 * rows, 128), BF16),
            pltpu.VMEM((chunks, 2 * rows, 128), F32),
            pltpu.VMEM((chunks, 2 * rows, 128), BF16),
            pltpu.VMEM((chunks, 2 * rows, 128), F32),
            pltpu.VMEM((chunks, 2 * rows, 256), F32),
            dma((1 + tiles + 5,)),
            dma((2 + chunks,)),
            dma((2 + chunks,)),
            dma((len(SENDS),)),
            dma((len(SENDS),)),
            dma((8,)),
            dma((8,)),
        ],
        compiler_params=pltpu.CompilerParams(
            collective_id=0, has_side_effects=True, vmem_limit_bytes=VMEM_LIMIT
        ),
        name="strand_attention",
    )(*(pltpu.with_memory_space_constraint(a, pltpu.HBM) for a in (tokens, w_same, w_partner, w_query, w_key, w_value.T)))
    return jnp.dot(mixed, w_out, preferred_element_type=F32).astype(BF16)[None]


def solution(mesh):
    placed = (P("ws", "seq", None), P(), P(), P(), P(), P(), P())
    return jax.shard_map(
        body, mesh=mesh, in_specs=placed, out_specs=P("ws", "seq", None), check_vma=False
    )
```

```python
import functools
import math

import jax
import jax.numpy as jnp
from jax import lax
from jax.experimental import pallas as pl
from jax.experimental.pallas import tpu as pltpu
from jax.sharding import PartitionSpec as P

MESH = pl.DeviceIdType.MESH
F32 = jnp.float32
BF16 = jnp.bfloat16
NT = (((1,), (1,)), ((), ()))
VMEM_LIMIT = 50 << 20
PIECE = 512
EARLY = 32

Y, H, M = 1, 2, 4
ORDER = (0, H, Y, M, Y ^ H, M ^ H, Y ^ M, Y ^ M ^ H)
PLACE = {slot: place for place, slot in enumerate(ORDER)}
SENDS = ((0, H, 0, 2), (0, Y, 0, 2), (0, M, 0, 2), (Y, H, 0, 2), (M, H, 0, 2), (M, Y, 0, 1), (Y, M, 1, 2), (Y ^ M, H, 0, 2))


def kernel(
    dims,
    tok, w_same, w_partner, w_query, w_key, w_value_t,
    out_ref,
    tok_v, same_v, partner_v, query_v, key_v, value_v, hid_v,
    kv_out, kv_in, kv_mine, kv_all, keys_v, vals_v,
    qb_out, qb_in, qa_v, q_v, peak_v, acc_v, tok_in,
    load_sem, pair_send, pair_recv, ring_send, ring_recv, core_send, core_recv,
):
    rows, width, heads, dk, dv = dims
    chunks = heads // 2
    half = rows // 2
    pack = 2 * rows + half
    ws = lax.axis_index("ws")
    seq = lax.axis_index("seq")
    last = lax.axis_size("seq") - 1
    x, y, core = seq // 4, (seq // 2) % 2, seq % 2
    pair = {"ws": ws + 1 - 2 * (ws % 2), "seq": last - seq}
    other = {"ws": ws, "seq": seq + 1 - 2 * core}
    link = {
        Y: {"ws": ws, "seq": seq + 2 - 4 * y},
        H: {"ws": ws, "seq": seq + 4 - 8 * (x % 2)},
        M: {"ws": ws, "seq": (3 - x) * 4 + y * 2 + core},
    }

    tiles = width // PIECE
    tail_rows = dv - 128
    sources = [(tok.at[0], tok_v)]
    sources += [(w_partner.at[:, pl.ds(n * PIECE, PIECE)], partner_v.at[n]) for n in range(tiles)]
    sources += [
        (w_key, key_v),
        (w_value_t, value_v.at[pl.ds(0, dv)]),
        (w_value_t.at[pl.ds(128, tail_rows)], value_v.at[pl.ds(dv, tail_rows)]),
    ]
    sources += [(w_query, query_v), (w_same, same_v)]
    loads = [pltpu.make_async_copy(src, dst, load_sem.at[n]) for n, (src, dst) in enumerate(sources)]
    kv_base = 1 + tiles
    q_base = kv_base + 3
    s_base = q_base + 1

    def begin(first, stop):
        for copy in loads[first:stop]:
            copy.start()

    begin(0, q_base)
    barrier = pltpu.get_barrier_semaphore()
    for peer in (pair, other, link[Y], link[H], link[M]):
        pl.semaphore_signal(barrier, inc=1, device_id=peer, device_id_type=MESH)

    def to_pair(src, dst, n):
        return pltpu.make_async_remote_copy(
            src_ref=src, dst_ref=dst, send_sem=pair_send.at[n], recv_sem=pair_recv.at[n],
            device_id=pair, device_id_type=MESH,
        )

    tok_copy = to_pair(tok.at[0, pl.ds(rows - EARLY, EARLY)], tok_in, 2 + chunks)

    turned = lax.broadcasted_iota(jnp.int32, (rows, rows), 0) + lax.broadcasted_iota(jnp.int32, (rows, rows), 1)
    turn = jnp.where(turned == rows - 1, 1.0, 0.0).astype(BF16)

    def key(h):
        return jnp.dot(h, key_v[...], preferred_element_type=F32)

    def value(h):
        return lax.dot_general(h, value_v[...], NT, preferred_element_type=F32)

    def tail(v):
        lane = lax.broadcasted_iota(jnp.int32, (half, 128), 1)
        return jnp.where(lane < tail_rows, v[:half, 128:], v[half:, 128:])

    with jax.named_scope("w_tok"):
        loads[0].wait()
    with jax.named_scope("hB"):
        for n in range(tiles):
            loads[1 + n].wait()
            part = jnp.dot(tok_v[...], partner_v[n], preferred_element_type=F32)
            hid_v[:, n * PIECE:(n + 1) * PIECE] = part.astype(BF16)
            if n == 0:
                begin(q_base, s_base)
                with jax.named_scope("barrier"):
                    pl.semaphore_wait(barrier, 5)
                tok_copy.start()
    begin(s_base, len(loads))
    kv_parts = (pl.ds(0, rows), pl.ds(rows, pack - rows))
    kv_copies = [to_pair(kv_out.at[part], kv_in.at[part], n) for n, part in enumerate(kv_parts)]
    sent = pl.ds(EARLY, rows - EARLY)
    q_copies = [to_pair(qb_out.at[n, :, sent], qb_in.at[n, :, sent], 2 + n) for n in range(chunks)]
    with jax.named_scope("kB"):
        for n in range(3):
            loads[kv_base + n].wait()
        kv_out[0:rows] = key(hid_v[...]).astype(BF16)
    kv_copies[0].start()
    with jax.named_scope("vB"):
        v = value(hid_v[...])
        kv_out[rows:2 * rows] = v[:, :128].astype(BF16)
        kv_out[2 * rows:] = tail(v).astype(BF16)
    kv_copies[1].start()

    def heads_of(q):
        for n in range(heads):
            yield n // 2, n % 2, q[:, n * dk:(n + 1) * dk]

    with jax.named_scope("qB"):
        loads[q_base].wait()
        q = jnp.dot(hid_v[...], query_v[...], preferred_element_type=F32).astype(BF16)
        q = jnp.dot(turn, q, preferred_element_type=F32).astype(BF16)
        for n, h, part in heads_of(q):
            qb_out[n, h] = part

    with jax.named_scope("hA"):
        loads[s_base].wait()
        q_copies[0].start()
        hid_v[...] = jnp.dot(tok_v[...], same_v[...], preferred_element_type=F32).astype(BF16)
    with jax.named_scope("kvA"):
        turned_hid = jnp.dot(turn, hid_v[...], preferred_element_type=F32).astype(BF16)
        kv_mine[0:rows] = key(turned_hid)
        v = value(turned_hid)
        kv_mine[rows:2 * rows] = v[:, :128]
        kv_mine[2 * rows:] = tail(v)
    with jax.named_scope("qA"):
        q = jnp.dot(hid_v[...], query_v[...], preferred_element_type=F32)
        for n, h, part in heads_of(q):
            qa_v[n, h] = part

    with jax.named_scope("w_kv"):
        for copy in kv_copies:
            copy.wait_recv()
    kv_all[0, 0] = (kv_mine[...] + kv_in[...].astype(F32)).astype(BF16)

    ring, came = {}, {slot: [] for slot in range(8)}
    for n, (slot, l, first, stop) in enumerate(SENDS):
        part = pl.ds(first * pack // 2, (stop - first) * pack // 2)
        ring[slot, l] = pltpu.make_async_remote_copy(
            src_ref=kv_all.at[slot, 0, part], dst_ref=kv_all.at[slot ^ l, 0, part],
            send_sem=ring_send.at[n], recv_sem=ring_recv.at[n],
            device_id=link[l], device_id_type=MESH,
        )
        came[slot ^ l].append(ring[slot, l])
    cores = {
        slot: pltpu.make_async_remote_copy(
            src_ref=kv_all.at[slot, 0], dst_ref=kv_all.at[slot, 1],
            send_sem=core_send.at[slot], recv_sem=core_recv.at[slot],
            device_id=other, device_id_type=MESH,
        )
        for slot in range(8)
    }

    def unpack(slot, c):
        place, at = PLACE[slot], c * rows
        if slot in (Y, M):
            place, at = 2 + c, rows * (slot == M)
        lane = lax.broadcasted_iota(jnp.int32, (half, 128), 1)
        keys_v[place, at:at + rows] = kv_all[slot, c, 0:rows]
        vals_v[place, at:at + rows, 0:128] = kv_all[slot, c, rows:2 * rows]
        t = kv_all[slot, c, 2 * rows:].astype(F32)
        ones = jnp.where(lane == tail_rows, 1.0, 0.0)
        first = jnp.where(lane < tail_rows, t, ones)
        second = jnp.where(lane < tail_rows, pltpu.roll(t, 64, 1), ones)
        vals_v[place, at:at + half, 128:256] = first.astype(BF16)
        vals_v[place, at + half:at + rows, 128:256] = second.astype(BF16)

    def arrive(slot, *onward):
        with jax.named_scope(f"w_slot{slot}"):
            for copy in came[slot]:
                copy.wait_recv()
        cores[slot].start()
        for l in onward:
            ring[slot, l].start()
        unpack(slot, 0)

    def complete(slot):
        with jax.named_scope(f"w_core{slot}"):
            cores[slot].wait_recv()
        unpack(slot, 1)

    def stage(place):
        if place == 0:
            complete(0)
        if place == 1:
            arrive(H)
            complete(H)
            arrive(Y, H)
            arrive(M, H)
            ring[M, Y].start()
            ring[Y, M].start()
            q_copies[3].start()
        if place == 3:
            complete(Y)
            complete(M)

    scale = dk ** -0.5 * math.log2(math.e)

    def query(c):
        if isinstance(c, int):
            with jax.named_scope(f'w_q{c}'):
                q_copies[c].wait_recv()
        else:
            for n in range(1, chunks - 1):
                @pl.when(c == n)
                def _():
                    with jax.named_scope(f"w_q{n}"):
                        q_copies[n].wait_recv()
        q_v[c] = ((qa_v[c] + qb_in[c].astype(F32)) * scale).astype(BF16).reshape(2 * rows, dk)

    def attend(q, places, peak, acc):
        for place in places:
            for j in range(0, 2 * rows, 256):
                s = lax.dot_general(q, keys_v[place, j:j + 256], NT, preferred_element_type=F32)
                new = jnp.maximum(peak, jnp.broadcast_to(jnp.max(s, axis=1, keepdims=True), peak.shape))
                weights = jnp.concatenate([jnp.exp2(s[:, :128] - new), jnp.exp2(s[:, 128:] - new)], axis=1).astype(BF16)
                keep = jnp.exp2(peak - new)
                acc = acc * jnp.concatenate([keep, keep], axis=1) + jnp.dot(
                    weights, vals_v[place, j:j + 256], preferred_element_type=F32
                )
                peak = new
        return peak, acc

    unpack(0, 0)
    ring[0, H].start()
    ring[0, Y].start()
    ring[0, M].start()
    cores[0].start()
    q_copies[1].start()
    q_copies[2].start()

    with jax.named_scope("early_q"):
        tok_copy.wait_recv()
        for n in range(tiles):
            part = jnp.dot(tok_in[...], partner_v[n], preferred_element_type=F32)
            hid_v[0:EARLY, n * PIECE:(n + 1) * PIECE] = part.astype(BF16)
        q = jnp.dot(hid_v[0:EARLY], query_v[...], preferred_element_type=F32).astype(BF16)
        q = jnp.dot(turn[rows - EARLY:, 0:EARLY], q, preferred_element_type=F32).astype(BF16)
        for n, h, part in heads_of(q):
            qb_in[n, h, 0:EARLY] = part

    query(0)
    peak_v[0] = jnp.full(peak_v.shape[1:], -jnp.inf, F32)
    acc_v[0] = jnp.zeros(acc_v.shape[1:], F32)

    def early(place, carry):
        for n in range(4):
            @pl.when(place == n)
            def _():
                stage(n)
        with jax.named_scope("early"):
            peak_v[0], acc_v[0] = attend(q_v[0], (place,), peak_v[0], acc_v[0])
        return carry

    lax.fori_loop(0, 4, early, 0)

    def one(c, place):
        with jax.named_scope("one"):
            peak_v[c], acc_v[c] = attend(q_v[c], (place,), peak_v[c], acc_v[c])

    def begin_chunk(c, places):
        with jax.named_scope("near"):
            start = jnp.full(peak_v.shape[1:], -jnp.inf, F32), jnp.zeros(acc_v.shape[1:], F32)
            peak_v[c], acc_v[c] = attend(q_v[c], places, *start)

    def early_chunk(c, carry):
        query(c)
        begin_chunk(c, range(4))

        @pl.when(c == 1)
        def _():
            arrive(Y ^ H)
        return carry

    lax.fori_loop(1, chunks - 1, early_chunk, 0)
    arrive(Y ^ M, H)
    complete(Y ^ H)
    with jax.named_scope("ones"):
        for c in range(chunks - 1):
            peak_v[c], acc_v[c] = attend(q_v[c], (PLACE[Y ^ H],), peak_v[c], acc_v[c])
    arrive(M ^ H)
    query(chunks - 1)
    begin_chunk(chunks - 1, range(5))
    complete(M ^ H)
    complete(Y ^ M)
    arrive(Y ^ M ^ H)
    with jax.named_scope("two"):
        peak_v[0], acc_v[0] = attend(q_v[0], (5, 6), peak_v[0], acc_v[0])
    complete(Y ^ M ^ H)
    one(0, 7)

    def store(c, acc):
        mixed = acc * (1.0 / acc[:, dv:dv + 1])
        lane = lax.broadcasted_iota(jnp.int32, (rows, 128), 1)
        a, b = mixed[:rows], mixed[rows:]
        turned_b = pltpu.roll(b[:, :128], 64, 1)
        inner = jnp.where(lane < 64, a[:, 128:], turned_b)
        end = jnp.where(lane < 64, turned_b, pltpu.roll(b[:, 128:], 64, 1))
        at = pl.multiple_of(c * 2 * dv, 128)
        out_ref[:, pl.ds(at, 2 * dv)] = jnp.concatenate([a[:, :128], inner, end], axis=1).astype(BF16)

    def far(c, carry):
        with jax.named_scope("far"):
            store(c - 1, acc_v[c - 1])
            _, acc_v[c] = attend(q_v[c], range(5, 8), peak_v[c], acc_v[c])
        return carry

    lax.fori_loop(1, chunks, far, 0)
    store(chunks - 1, acc_v[chunks - 1])

    for copy in kv_copies + q_copies + [tok_copy]:
        copy.wait_send()
    for copy in ring.values():
        copy.wait_send()
    for copy in cores.values():
        copy.wait_send()


def body(tokens, w_same, w_partner, w_query, w_key, w_value, w_out):
    _, rows, width = tokens.shape
    dk, dv = w_key.shape[1], w_value.shape[1]
    heads = w_query.shape[1] // dk
    chunks, tiles, pack = heads // 2, width // PIECE, 2 * rows + rows // 2
    dma = pltpu.SemaphoreType.DMA
    in_hbm = pl.BlockSpec(memory_space=pltpu.HBM)
    mixed = pl.pallas_call(
        functools.partial(kernel, (rows, width, heads, dk, dv)),
        out_shape=jax.ShapeDtypeStruct((rows, heads * dv), BF16),
        in_specs=[in_hbm] * 6,
        out_specs=pl.BlockSpec(memory_space=pltpu.VMEM),
        scratch_shapes=[
            pltpu.VMEM((rows, width), BF16),
            pltpu.VMEM((width, width), BF16),
            pltpu.VMEM((tiles, width, PIECE), BF16),
            pltpu.VMEM((width, heads * dk), BF16),
            pltpu.VMEM((width, dk), BF16),
            pltpu.VMEM((256, width), BF16),
            pltpu.VMEM((rows, width), BF16),
            pltpu.VMEM((pack, 128), BF16),
            pltpu.VMEM((pack, 128), BF16),
            pltpu.VMEM((pack, 128), F32),
            pltpu.VMEM((8, 2, pack, 128), BF16),
            pltpu.VMEM((8, 2 * rows, 128), BF16),
            pltpu.VMEM((8, 2 * rows, 256), BF16),
            pltpu.VMEM((chunks, 2, rows, dk), BF16),
            pltpu.VMEM((chunks, 2, rows, dk), BF16),
            pltpu.VMEM((chunks, 2, rows, dk), F32),
            pltpu.VMEM((chunks, 2 * rows, 128), BF16),
            pltpu.VMEM((chunks, 2 * rows, 128), F32),
            pltpu.VMEM((chunks, 2 * rows, 256), F32),
            pltpu.VMEM((EARLY, width), BF16),
            dma((1 + tiles + 5,)),
            dma((3 + chunks,)),
            dma((3 + chunks,)),
            dma((len(SENDS),)),
            dma((len(SENDS),)),
            dma((8,)),
            dma((8,)),
        ],
        compiler_params=pltpu.CompilerParams(
            collective_id=0, has_side_effects=True, vmem_limit_bytes=VMEM_LIMIT
        ),
        name="strand_attention",
    )(*(pltpu.with_memory_space_constraint(a, pltpu.HBM) for a in (tokens, w_same, w_partner, w_query, w_key, w_value.T)))
    return jnp.dot(mixed, w_out, preferred_element_type=F32).astype(BF16)[None]


def solution(mesh):
    placed = (P("ws", "seq", None), P(), P(), P(), P(), P(), P())
    return jax.shard_map(
        body, mesh=mesh, in_specs=placed, out_specs=P("ws", "seq", None), check_vma=False
    )
```

```python
import functools
import math

import jax
import jax.numpy as jnp
from jax import lax
from jax.experimental import pallas as pl
from jax.experimental.pallas import tpu as pltpu
from jax.sharding import PartitionSpec as P

MESH = pl.DeviceIdType.MESH
F32 = jnp.float32
BF16 = jnp.bfloat16
NT = (((1,), (1,)), ((), ()))
VMEM_LIMIT = 50 << 20
PIECE = 512
EARLY = 32

Y, H, M = 1, 2, 4
ORDER = (0, H, Y, M, Y ^ H, M ^ H, Y ^ M, Y ^ M ^ H)
PLACE = {slot: place for place, slot in enumerate(ORDER)}
SENDS = ((0, H, 0, 2), (0, Y, 0, 2), (0, M, 0, 2), (Y, H, 0, 2), (M, H, 0, 2), (M, Y, 0, 1), (Y, M, 1, 2), (Y ^ M, H, 0, 2))


def kernel(
    dims,
    tok, w_same, w_partner, w_query, w_key, w_value_t,
    out_ref,
    tok_v, same_v, partner_v, query_v, key_v, value_v, hid_v,
    kv_out, kv_in, kv_mine, kv_all, keys_v, vals_v,
    qb_out, qb_in, qa_v, q_v, peak_v, acc_v, tok_in,
    load_sem, pair_send, pair_recv, ring_send, ring_recv, core_send, core_recv,
):
    rows, width, heads, dk, dv = dims
    chunks = heads // 2
    half = rows // 2
    pack = 2 * rows + half
    ws = lax.axis_index("ws")
    seq = lax.axis_index("seq")
    last = lax.axis_size("seq") - 1
    x, y, core = seq // 4, (seq // 2) % 2, seq % 2
    pair = {"ws": ws + 1 - 2 * (ws % 2), "seq": last - seq}
    other = {"ws": ws, "seq": seq + 1 - 2 * core}
    link = {
        Y: {"ws": ws, "seq": seq + 2 - 4 * y},
        H: {"ws": ws, "seq": seq + 4 - 8 * (x % 2)},
        M: {"ws": ws, "seq": (3 - x) * 4 + y * 2 + core},
    }

    tiles = width // PIECE
    tail_rows = dv - 128
    sources = [(tok.at[0], tok_v)]
    sources += [(w_partner.at[:, pl.ds(n * PIECE, PIECE)], partner_v.at[n]) for n in range(tiles)]
    sources += [
        (w_key, key_v),
        (w_value_t, value_v.at[pl.ds(0, dv)]),
        (w_value_t.at[pl.ds(128, tail_rows)], value_v.at[pl.ds(dv, tail_rows)]),
    ]
    sources += [(w_query, query_v), (w_same, same_v)]
    loads = [pltpu.make_async_copy(src, dst, load_sem.at[n]) for n, (src, dst) in enumerate(sources)]
    kv_base = 1 + tiles
    q_base = kv_base + 3
    s_base = q_base + 1

    def begin(first, stop):
        for copy in loads[first:stop]:
            copy.start()

    begin(0, q_base)
    barrier = pltpu.get_barrier_semaphore()
    for peer in (pair, other, link[Y], link[H], link[M]):
        pl.semaphore_signal(barrier, inc=1, device_id=peer, device_id_type=MESH)

    def to_pair(src, dst, n):
        return pltpu.make_async_remote_copy(
            src_ref=src, dst_ref=dst, send_sem=pair_send.at[n], recv_sem=pair_recv.at[n],
            device_id=pair, device_id_type=MESH,
        )

    tok_copy = to_pair(tok.at[0, pl.ds(rows - EARLY, EARLY)], tok_in, 2 + chunks)

    turned = lax.broadcasted_iota(jnp.int32, (rows, rows), 0) + lax.broadcasted_iota(jnp.int32, (rows, rows), 1)
    turn = jnp.where(turned == rows - 1, 1.0, 0.0).astype(BF16)

    def key(h):
        return jnp.dot(h, key_v[...], preferred_element_type=F32)

    def value(h):
        return lax.dot_general(h, value_v[...], NT, preferred_element_type=F32)

    def tail(v):
        lane = lax.broadcasted_iota(jnp.int32, (half, 128), 1)
        return jnp.where(lane < tail_rows, v[:half, 128:], v[half:, 128:])

    with jax.named_scope("w_tok"):
        loads[0].wait()
    with jax.named_scope("hB"):
        for n in range(tiles):
            loads[1 + n].wait()
            part = jnp.dot(tok_v[...], partner_v[n], preferred_element_type=F32)
            hid_v[:, n * PIECE:(n + 1) * PIECE] = part.astype(BF16)
            if n == 1:
                begin(q_base, s_base)
            if n == 0:
                with jax.named_scope("barrier"):
                    pl.semaphore_wait(barrier, 5)
                tok_copy.start()
    begin(s_base, len(loads))
    kv_parts = (pl.ds(0, rows), pl.ds(rows, pack - rows))
    kv_copies = [to_pair(kv_out.at[part], kv_in.at[part], n) for n, part in enumerate(kv_parts)]
    sent = pl.ds(EARLY, rows - EARLY)
    q_copies = [to_pair(qb_out.at[n, :, sent], qb_in.at[n, :, sent], 2 + n) for n in range(chunks)]
    with jax.named_scope("kB"):
        for n in range(3):
            loads[kv_base + n].wait()
        kv_out[0:rows] = key(hid_v[...]).astype(BF16)
    kv_copies[0].start()
    with jax.named_scope("vB"):
        v = value(hid_v[...])
        kv_out[rows:2 * rows] = v[:, :128].astype(BF16)
        kv_out[2 * rows:] = tail(v).astype(BF16)
    kv_copies[1].start()

    def heads_of(q):
        for n in range(heads):
            yield n // 2, n % 2, q[:, n * dk:(n + 1) * dk]

    with jax.named_scope("qB"):
        loads[q_base].wait()
        q = jnp.dot(hid_v[...], query_v[...], preferred_element_type=F32).astype(BF16)
        q = jnp.dot(turn, q, preferred_element_type=F32).astype(BF16)
        for n, h, part in heads_of(q):
            qb_out[n, h] = part

    with jax.named_scope("hA"):
        loads[s_base].wait()
        q_copies[0].start()
        hid_v[...] = jnp.dot(tok_v[...], same_v[...], preferred_element_type=F32).astype(BF16)
    with jax.named_scope("kvA"):
        turned_hid = jnp.dot(turn, hid_v[...], preferred_element_type=F32).astype(BF16)
        kv_mine[0:rows] = key(turned_hid)
        v = value(turned_hid)
        kv_mine[rows:2 * rows] = v[:, :128]
        kv_mine[2 * rows:] = tail(v)
    with jax.named_scope("qA"):
        q = jnp.dot(hid_v[...], query_v[...], preferred_element_type=F32)
        for n, h, part in heads_of(q):
            qa_v[n, h] = part

    with jax.named_scope("w_kv"):
        for copy in kv_copies:
            copy.wait_recv()
    kv_all[0, 0] = (kv_mine[...] + kv_in[...].astype(F32)).astype(BF16)

    ring, came = {}, {slot: [] for slot in range(8)}
    for n, (slot, l, first, stop) in enumerate(SENDS):
        part = pl.ds(first * pack // 2, (stop - first) * pack // 2)
        ring[slot, l] = pltpu.make_async_remote_copy(
            src_ref=kv_all.at[slot, 0, part], dst_ref=kv_all.at[slot ^ l, 0, part],
            send_sem=ring_send.at[n], recv_sem=ring_recv.at[n],
            device_id=link[l], device_id_type=MESH,
        )
        came[slot ^ l].append(ring[slot, l])
    cores = {
        slot: pltpu.make_async_remote_copy(
            src_ref=kv_all.at[slot, 0], dst_ref=kv_all.at[slot, 1],
            send_sem=core_send.at[slot], recv_sem=core_recv.at[slot],
            device_id=other, device_id_type=MESH,
        )
        for slot in range(8)
    }

    def unpack(slot, c):
        place, at = PLACE[slot], c * rows
        if slot in (Y, M):
            place, at = 2 + c, rows * (slot == M)
        lane = lax.broadcasted_iota(jnp.int32, (half, 128), 1)
        keys_v[place, at:at + rows] = kv_all[slot, c, 0:rows]
        vals_v[place, at:at + rows, 0:128] = kv_all[slot, c, rows:2 * rows]
        t = kv_all[slot, c, 2 * rows:].astype(F32)
        ones = jnp.where(lane == tail_rows, 1.0, 0.0)
        first = jnp.where(lane < tail_rows, t, ones)
        second = jnp.where(lane < tail_rows, pltpu.roll(t, 64, 1), ones)
        vals_v[place, at:at + half, 128:256] = first.astype(BF16)
        vals_v[place, at + half:at + rows, 128:256] = second.astype(BF16)

    def arrive(slot, *onward):
        with jax.named_scope(f"w_slot{slot}"):
            for copy in came[slot]:
                copy.wait_recv()
        cores[slot].start()
        for l in onward:
            ring[slot, l].start()
        unpack(slot, 0)

    def complete(slot):
        with jax.named_scope(f"w_core{slot}"):
            cores[slot].wait_recv()
        unpack(slot, 1)

    def stage(place):
        if place == 0:
            complete(0)
        if place == 1:
            arrive(H)
            complete(H)
            arrive(Y, H)
            arrive(M, H)
            ring[M, Y].start()
            ring[Y, M].start()
            q_copies[3].start()
        if place == 3:
            complete(Y)
            complete(M)

    scale = dk ** -0.5 * math.log2(math.e)

    def query(c):
        if isinstance(c, int):
            with jax.named_scope(f'w_q{c}'):
                q_copies[c].wait_recv()
        else:
            for n in range(1, chunks - 1):
                @pl.when(c == n)
                def _():
                    with jax.named_scope(f"w_q{n}"):
                        q_copies[n].wait_recv()
        q_v[c] = ((qa_v[c] + qb_in[c].astype(F32)) * scale).astype(BF16).reshape(2 * rows, dk)

    def attend(q, places, peak, acc):
        for place in places:
            for j in range(0, 2 * rows, 256):
                s = lax.dot_general(q, keys_v[place, j:j + 256], NT, preferred_element_type=F32)
                new = jnp.maximum(peak, jnp.broadcast_to(jnp.max(s, axis=1, keepdims=True), peak.shape))
                weights = jnp.concatenate([jnp.exp2(s[:, :128] - new), jnp.exp2(s[:, 128:] - new)], axis=1).astype(BF16)
                keep = jnp.exp2(peak - new)
                acc = acc * jnp.concatenate([keep, keep], axis=1) + jnp.dot(
                    weights, vals_v[place, j:j + 256], preferred_element_type=F32
                )
                peak = new
        return peak, acc

    unpack(0, 0)
    ring[0, H].start()
    ring[0, Y].start()
    ring[0, M].start()
    cores[0].start()
    q_copies[1].start()
    q_copies[2].start()

    with jax.named_scope("early_q"):
        tok_copy.wait_recv()
        for n in range(tiles):
            part = jnp.dot(tok_in[...], partner_v[n], preferred_element_type=F32)
            hid_v[0:EARLY, n * PIECE:(n + 1) * PIECE] = part.astype(BF16)
        q = jnp.dot(hid_v[0:EARLY], query_v[...], preferred_element_type=F32).astype(BF16)
        q = jnp.dot(turn[rows - EARLY:, 0:EARLY], q, preferred_element_type=F32).astype(BF16)
        for n, h, part in heads_of(q):
            qb_in[n, h, 0:EARLY] = part

    query(0)
    peak_v[0] = jnp.full(peak_v.shape[1:], -jnp.inf, F32)
    acc_v[0] = jnp.zeros(acc_v.shape[1:], F32)

    def early(place, carry):
        for n in range(4):
            @pl.when(place == n)
            def _():
                stage(n)
        with jax.named_scope("early"):
            peak_v[0], acc_v[0] = attend(q_v[0], (place,), peak_v[0], acc_v[0])
        return carry

    lax.fori_loop(0, 4, early, 0)

    def one(c, place):
        with jax.named_scope("one"):
            peak_v[c], acc_v[c] = attend(q_v[c], (place,), peak_v[c], acc_v[c])

    def begin_chunk(c, places):
        with jax.named_scope("near"):
            start = jnp.full(peak_v.shape[1:], -jnp.inf, F32), jnp.zeros(acc_v.shape[1:], F32)
            peak_v[c], acc_v[c] = attend(q_v[c], places, *start)

    def early_chunk(c, carry):
        query(c)
        begin_chunk(c, range(4))

        @pl.when(c == 1)
        def _():
            arrive(Y ^ H)
        return carry

    lax.fori_loop(1, chunks - 1, early_chunk, 0)
    arrive(Y ^ M, H)
    complete(Y ^ H)
    with jax.named_scope("ones"):
        for c in range(chunks - 1):
            peak_v[c], acc_v[c] = attend(q_v[c], (PLACE[Y ^ H],), peak_v[c], acc_v[c])
    arrive(M ^ H)
    query(chunks - 1)
    begin_chunk(chunks - 1, range(5))
    complete(M ^ H)
    complete(Y ^ M)
    arrive(Y ^ M ^ H)
    with jax.named_scope("two"):
        for c in range(2):
            peak_v[c], acc_v[c] = attend(q_v[c], (5, 6), peak_v[c], acc_v[c])
    complete(Y ^ M ^ H)
    with jax.named_scope("one"):
        for c in range(2):
            _, acc_v[c] = attend(q_v[c], (7,), peak_v[c], acc_v[c])

    def store(c, acc):
        mixed = acc * (1.0 / acc[:, dv:dv + 1])
        lane = lax.broadcasted_iota(jnp.int32, (rows, 128), 1)
        a, b = mixed[:rows], mixed[rows:]
        turned_b = pltpu.roll(b[:, :128], 64, 1)
        inner = jnp.where(lane < 64, a[:, 128:], turned_b)
        end = jnp.where(lane < 64, turned_b, pltpu.roll(b[:, 128:], 64, 1))
        at = pl.multiple_of(c * 2 * dv, 128)
        out_ref[:, pl.ds(at, 2 * dv)] = jnp.concatenate([a[:, :128], inner, end], axis=1).astype(BF16)

    def far(c, carry):
        with jax.named_scope("far"):
            store(c - 1, acc_v[c - 1])
            _, acc_v[c] = attend(q_v[c], range(5, 8), peak_v[c], acc_v[c])
        return carry

    store(0, acc_v[0])
    lax.fori_loop(2, chunks, far, 0)
    store(chunks - 1, acc_v[chunks - 1])

    for copy in kv_copies + q_copies + [tok_copy]:
        copy.wait_send()
    for copy in ring.values():
        copy.wait_send()
    for copy in cores.values():
        copy.wait_send()


def body(tokens, w_same, w_partner, w_query, w_key, w_value, w_out):
    _, rows, width = tokens.shape
    dk, dv = w_key.shape[1], w_value.shape[1]
    heads = w_query.shape[1] // dk
    chunks, tiles, pack = heads // 2, width // PIECE, 2 * rows + rows // 2
    dma = pltpu.SemaphoreType.DMA
    in_hbm = pl.BlockSpec(memory_space=pltpu.HBM)
    mixed = pl.pallas_call(
        functools.partial(kernel, (rows, width, heads, dk, dv)),
        out_shape=jax.ShapeDtypeStruct((rows, heads * dv), BF16),
        in_specs=[in_hbm] * 6,
        out_specs=pl.BlockSpec(memory_space=pltpu.VMEM),
        scratch_shapes=[
            pltpu.VMEM((rows, width), BF16),
            pltpu.VMEM((width, width), BF16),
            pltpu.VMEM((tiles, width, PIECE), BF16),
            pltpu.VMEM((width, heads * dk), BF16),
            pltpu.VMEM((width, dk), BF16),
            pltpu.VMEM((256, width), BF16),
            pltpu.VMEM((rows, width), BF16),
            pltpu.VMEM((pack, 128), BF16),
            pltpu.VMEM((pack, 128), BF16),
            pltpu.VMEM((pack, 128), F32),
            pltpu.VMEM((8, 2, pack, 128), BF16),
            pltpu.VMEM((8, 2 * rows, 128), BF16),
            pltpu.VMEM((8, 2 * rows, 256), BF16),
            pltpu.VMEM((chunks, 2, rows, dk), BF16),
            pltpu.VMEM((chunks, 2, rows, dk), BF16),
            pltpu.VMEM((chunks, 2, rows, dk), F32),
            pltpu.VMEM((chunks, 2 * rows, 128), BF16),
            pltpu.VMEM((chunks, 2 * rows, 128), F32),
            pltpu.VMEM((chunks, 2 * rows, 256), F32),
            pltpu.VMEM((EARLY, width), BF16),
            dma((1 + tiles + 5,)),
            dma((3 + chunks,)),
            dma((3 + chunks,)),
            dma((len(SENDS),)),
            dma((len(SENDS),)),
            dma((8,)),
            dma((8,)),
        ],
        compiler_params=pltpu.CompilerParams(
            collective_id=0, has_side_effects=True, vmem_limit_bytes=VMEM_LIMIT
        ),
        name="strand_attention",
    )(*(pltpu.with_memory_space_constraint(a, pltpu.HBM) for a in (tokens, w_same, w_partner, w_query, w_key, w_value.T)))
    return jnp.dot(mixed, w_out, preferred_element_type=F32).astype(BF16)[None]


def solution(mesh):
    placed = (P("ws", "seq", None), P(), P(), P(), P(), P(), P())
    return jax.shard_map(
        body, mesh=mesh, in_specs=placed, out_specs=P("ws", "seq", None), check_vma=False
    )
```
